32 devices in a mesh: freq: 8 (over y, x, core), rcv: 4 (over z).
Axes of the slice: x: 2, y: 2, z: 4, core: 2. Of those that a mesh axis runs over, the one named last changes fastest.
Arguments:
- green_freq: float32 [2, 8, 2304, 2304], P(None, 'freq', 'rcv'), may hold values from -6 to 6
- data_matrix: float32 [2, 8, 2304, 2304], P(None, 'freq', 'rcv'), may hold values from -0.09375 to 0.09375
- shot_panels: float32 [2, 8, 2304, 256], P(None, 'freq', 'rcv'), may hold values from -6 to 6
- wavelet: float32 [2, 8], P(None, 'freq'), may hold values from -1.5 to 1.5
- sources: int32 [256], replicated, may hold values from 0 to 2303, as said below
- support: int32 [8, 2304], replicated, may hold values 0 or 1
- threshold: float32 [1], replicated, may hold values from 3 to 7
Outputs:
- green_next: float32 [2, 8, 2304, 2304], P(None, 'freq', 'rcv')
- residual: float32 [2, 8, 2304, 256], P(None, 'freq', 'rcv')
The draws below stay inside these ranges and needn't reach their ends.
Inputs may be any that keep to these rules, and one draw needn't show every extreme that they name: `sources`: 256 distinct source positions. `support`: a 0/1 mask over time samples and source positions.
All inputs are finite; a program needn't handle non-finite values.
Results may differ from the reference program's by a relative error of at most 0.00013.
Values sent between devices are 32-bit elements; how exact they have to be, the bound alone decides.
A program may use at most 128 MiB of HBM per device.

```python
import math
import jax
import jax.numpy as jnp
from jax import lax

NGRID = 2304
NC = 256
NF = 8


def draw_sources(key, part):
    order = jax.random.permutation(jax.random.fold_in(key, 11), NGRID)
    return order[:NC].astype(jnp.int32)


def place_ends(entries, stream_key, smallest, high):
    place = [jax.random.randint(jax.random.fold_in(stream_key, axis), (), 0, length) for axis, length in enumerate(entries.shape)]
    longest = entries.shape.index(max(entries.shape))
    neighbour = place[:longest] + [(place[longest] + 1) % entries.shape[longest]] + place[longest + 1:]
    return entries.at[tuple(place)].set(smallest).at[tuple(neighbour)].set(high)


def steps_of(rng, shape, pieces, least, largest):
    gain = 1.0
    for position, parts in pieces:
        steps = jax.random.uniform(jax.random.fold_in(jax.random.fold_in(rng, 6), position), (parts,), jnp.float32, least / len(pieces), largest / len(pieces))
        gain = gain * jnp.repeat(jnp.exp(steps), shape[position] // parts).reshape((-1,) + (1,) * (len(shape) - 1 - position))
    return gain


def normal_values(key, shape, width, most, cuts=(), kind=jnp.bfloat16):
    array = jax.random.normal(key, shape, jnp.float32) * width
    if len(cuts) > 0:
        array = steps_of(key, shape, cuts, -0.22, 0.18) * array
    return jnp.clip(array, min=-most, max=most).astype(kind)


def setup_inputs(seed: int = 0) -> dict:
    key_list = jax.random.split(jax.random.key(seed), 8)
    green_freq = normal_values(key_list[0], (2, NF, NGRID, NGRID), 1.0, 6.0, ((1, 8), (2, 4)), jnp.float32)
    data_matrix = normal_values(key_list[1], (2, NF, NGRID, NGRID), (2 * NGRID) ** -0.5, 0.09375, ((1, 8), (2, 4)), jnp.float32)
    shot_panels = normal_values(key_list[2], (2, NF, NGRID, NC), 1.0, 6.0, ((1, 8), (2, 4)), jnp.float32)
    wavelet = jnp.clip(jax.random.uniform(key_list[3], (2, NF), jnp.float32, -1.5, 1.5) * steps_of(key_list[3], (2, NF), ((1, 8),), -0.4, 0.0), -1.5, 1.5)
    sources = draw_sources(jax.random.fold_in(key_list[7], 71), 0)
    support = place_ends((jax.random.randint(key_list[5], (NF, NGRID), 0, 4) < 3).astype(jnp.int32), jax.random.fold_in(key_list[5], 1), 0, 1)
    threshold = jnp.clip(jax.random.uniform(key_list[6], (1,), jnp.float32, 3.0, 7.0), 3.0, 7.0)
    return {"green_freq": green_freq, "data_matrix": data_matrix, "shot_panels": shot_panels, "wavelet": wavelet, "sources": sources, "support": support, "threshold": threshold}


HIGHEST = lax.Precision.HIGHEST

def complex_product(left_pair, right_pair, pattern):
    left_real, left_imag = left_pair
    right_real, right_imag = right_pair
    real_part = jnp.einsum(pattern, left_real, right_real, precision=HIGHEST) - jnp.einsum(pattern, left_imag, right_imag, precision=HIGHEST)
    imag_part = jnp.einsum(pattern, left_real, right_imag, precision=HIGHEST) + jnp.einsum(pattern, left_imag, right_real, precision=HIGHEST)
    return (real_part, imag_part)

def conj_product(left_pair, right_pair, pattern):
    left_real, left_imag = left_pair
    right_real, right_imag = right_pair
    real_part = jnp.einsum(pattern, left_real, right_real, precision=HIGHEST) + jnp.einsum(pattern, left_imag, right_imag, precision=HIGHEST)
    imag_part = jnp.einsum(pattern, left_real, right_imag, precision=HIGHEST) - jnp.einsum(pattern, left_imag, right_real, precision=HIGHEST)
    return (real_part, imag_part)

def shrink_spectra(spectra, keep, shrink_level):
    n_freq = spectra.shape[1]
    grid = jnp.arange(n_freq, dtype=jnp.int32)
    phase = grid[:, None] * grid[None, :] % n_freq
    angle = phase.astype(jnp.float32) * (2.0 * math.pi / n_freq)
    cos_table = jnp.cos(angle)
    sin_table = jnp.sin(angle)
    pattern = 'tf,f...->t...'
    time_real = jnp.einsum(pattern, cos_table, spectra[0], precision=HIGHEST) - jnp.einsum(pattern, sin_table, spectra[1], precision=HIGHEST)
    time_imag = jnp.einsum(pattern, sin_table, spectra[0], precision=HIGHEST) + jnp.einsum(pattern, cos_table, spectra[1], precision=HIGHEST)
    magnitude = jnp.sqrt(time_real * time_real + time_imag * time_imag)
    factor = jnp.maximum(magnitude - shrink_level, 0.0) / jnp.maximum(magnitude, shrink_level) * keep
    kept_real = factor * time_real
    kept_imag = factor * time_imag
    back_real = (jnp.einsum(pattern, cos_table, kept_real, precision=HIGHEST) + jnp.einsum(pattern, sin_table, kept_imag, precision=HIGHEST)) / n_freq
    back_imag = (jnp.einsum(pattern, cos_table, kept_imag, precision=HIGHEST) - jnp.einsum(pattern, sin_table, kept_real, precision=HIGHEST)) / n_freq
    return jnp.stack([back_real, back_imag])

def reference(green_freq, data_matrix, shot_panels, wavelet, sources, support, threshold):
    picked = jnp.take(green_freq, sources, axis=3)

    def per_frequency(inputs):
        green_cols, data_now, shots_now, wave_now = inputs
        wave_real = wave_now[0]
        wave_imag = wave_now[1]
        data_pair = (data_now[0], data_now[1])
        multiple = complex_product(data_pair, (green_cols[0], green_cols[1]), 'rk,kc->rc')
        resid_real = shots_now[0] - (wave_real * green_cols[0] - wave_imag * green_cols[1] - multiple[0])
        resid_imag = shots_now[1] - (wave_real * green_cols[1] + wave_imag * green_cols[0] - multiple[1])
        adjoint = conj_product(data_pair, (resid_real, resid_imag), 'rk,rc->kc')
        dir_real = wave_real * resid_real + wave_imag * resid_imag - adjoint[0]
        dir_imag = wave_real * resid_imag - wave_imag * resid_real - adjoint[1]
        pushed = complex_product(data_pair, (dir_real, dir_imag), 'rk,kc->rc')
        image_real = wave_real * dir_real - wave_imag * dir_imag - pushed[0]
        image_imag = wave_real * dir_imag + wave_imag * dir_real - pushed[1]
        norm_dir = jnp.sum(dir_real * dir_real + dir_imag * dir_imag)
        norm_img = jnp.sum(image_real * image_real + image_imag * image_imag)
        return (jnp.stack([resid_real, resid_imag]), jnp.stack([dir_real, dir_imag]), norm_dir, norm_img)
    mapped = lax.map(per_frequency, (jnp.moveaxis(picked, 1, 0), jnp.moveaxis(data_matrix, 1, 0), jnp.moveaxis(shot_panels, 1, 0), jnp.moveaxis(wavelet, 1, 0)))
    residual = jnp.moveaxis(mapped[0], 0, 1)
    direction = jnp.moveaxis(mapped[1], 0, 1)
    step_size = jnp.sum(mapped[2]) / jnp.sum(mapped[3])
    updated = green_freq.at[:, :, :, sources].add(step_size * direction)
    rows_first = jnp.moveaxis(updated, 2, 0)
    keep = support.astype(jnp.float32)

    def shrink_row(spectra_row):
        return shrink_spectra(spectra_row, keep, threshold[0])
    shrunk = lax.map(shrink_row, rows_first)
    green_next = jnp.moveaxis(shrunk, 0, 2)
    return (green_next, residual)
```

```python
import functools
import math

import jax
import jax.numpy as jnp
from jax import lax
from jax.experimental import pallas as pl
from jax.experimental.pallas import tpu as pltpu
from jax.sharding import PartitionSpec as P

HIGH = lax.Precision.HIGH
MESH = pl.DeviceIdType.MESH


def transform(points, sign):
    count = len(points)
    if count == 1:
        return points
    if count % 2:
        out = []
        for t in range(count):
            real, imag = points[0]
            for f in range(1, count):
                angle = sign * 2.0 * math.pi * (f * t % count) / count
                c, s = math.cos(angle), math.sin(angle)
                real = real + (c * points[f][0] - s * points[f][1])
                imag = imag + (s * points[f][0] + c * points[f][1])
            out.append((real, imag))
        return out
    even = transform(points[0::2], sign)
    odd = transform(points[1::2], sign)
    low, high = [], []
    for k in range(count // 2):
        er, ei = even[k]
        r, i = odd[k]
        angle = 8 * k / count
        if k == 0:
            tr, ti = r, i
        elif angle == 2:
            tr, ti = (-i, r) if sign > 0 else (i, -r)
        elif angle == 1:
            h = math.sqrt(0.5)
            tr, ti = (h * (r - i), h * (r + i)) if sign > 0 else (h * (r + i), h * (i - r))
        elif angle == 3:
            h = math.sqrt(0.5)
            tr, ti = (-h * (r + i), h * (r - i)) if sign > 0 else (h * (i - r), -h * (r + i))
        else:
            c = math.cos(2 * math.pi * k / count)
            s = sign * math.sin(2 * math.pi * k / count)
            tr, ti = c * r - s * i, s * r + c * i
        low.append((er + tr, ei + ti))
        high.append((er - tr, ei - ti))
    return low + high


def shrink_points(points, keep, level):
    count = len(points)
    timed = transform(points, 1)
    kept = []
    for t, (real, imag) in enumerate(timed):
        size = jnp.sqrt(real * real + imag * imag)
        factor = jnp.maximum(size - level, 0.0) / jnp.maximum(size, level) * keep[t : t + 1]
        factor = factor * (1.0 / count)
        kept.append((factor * real, factor * imag))
    return transform(kept, -1)


def shrink_body(scal_ref, keep_ref, *refs):
    *x_refs, o_ref = refs
    x_ref = x_refs[0]
    count = x_ref.shape[1]
    level = scal_ref[0]

    def lanes(j, carry):
        at = pl.ds(pl.multiple_of(j * 128, 128), 128)
        points = [(x_ref[0, f, :, at], x_ref[1, f, :, at]) for f in range(count)]
        if len(x_refs) == 2:
            d_ref = x_refs[1]
            step = scal_ref[1]
            points = [
                (r + step * d_ref[0, f, :, at], i + step * d_ref[1, f, :, at])
                for f, (r, i) in enumerate(points)
            ]
        out = shrink_points(points, keep_ref[:, at], level)
        for f in range(count):
            o_ref[0, f, :, at] = out[f][0]
            o_ref[1, f, :, at] = out[f][1]
        return carry

    lax.fori_loop(0, x_ref.shape[3] // 128, lanes, 0)


def shrink_call(scalars, keep, arrays):
    two, count, rows, width = arrays[0].shape
    tile = 8 if rows % 8 == 0 else rows
    if rows % 24 == 0 and width <= 512:
        tile = 24
    block = pl.BlockSpec((two, count, tile, width), lambda j: (0, 0, j, 0))
    size = arrays[0].size * 4
    return pl.pallas_call(
        shrink_body,
        grid=(rows // tile,),
        in_specs=[
            pl.BlockSpec(memory_space=pltpu.SMEM),
            pl.BlockSpec((count, width), lambda j: (0, 0)),
        ]
        + [block] * len(arrays),
        out_specs=block,
        out_shape=jax.ShapeDtypeStruct(arrays[0].shape, jnp.float32),
        cost_estimate=pl.CostEstimate(
            flops=40 * arrays[0].size, bytes_accessed=size * (1 + len(arrays)), transcendentals=0
        ),
    )(scalars, keep, *arrays)


def merge_body(mask_ref, hot_ref, cols_ref, back_ref, o_ref):
    hot = hot_ref[...]
    mask = mask_ref[...] > 0.5
    for part in range(2):
        x = cols_ref[:, part * hot.shape[0] : (part + 1) * hot.shape[0]]
        hi = x.astype(jnp.bfloat16)
        rest = x - hi.astype(jnp.float32)
        mid = rest.astype(jnp.bfloat16)
        low = (rest - mid.astype(jnp.float32)).astype(jnp.bfloat16)
        spread = (
            jnp.dot(hi, hot, preferred_element_type=jnp.float32)
            + jnp.dot(mid, hot, preferred_element_type=jnp.float32)
        ) + jnp.dot(low, hot, preferred_element_type=jnp.float32)
        o_ref[part, 0] = jnp.where(mask, spread, back_ref[part, 0])


def merge_call(mask, hot, cols, back):
    two, one, rows, width = back.shape
    picked = hot.shape[0]
    tile = rows // 4 if rows % 32 == 0 else rows
    return pl.pallas_call(
        merge_body,
        grid=(rows // tile,),
        in_specs=[
            pl.BlockSpec((1, width), lambda i: (0, 0)),
            pl.BlockSpec((picked, width), lambda i: (0, 0)),
            pl.BlockSpec((tile, two * picked), lambda i: (i, 0)),
            pl.BlockSpec((two, one, tile, width), lambda i: (0, 0, i, 0)),
        ],
        out_specs=pl.BlockSpec((two, one, tile, width), lambda i: (0, 0, i, 0)),
        out_shape=jax.ShapeDtypeStruct(back.shape, jnp.float32),
    )(mask, hot, cols, back)


def dots(lhs, rhs, contract):
    return lax.dot_general(lhs, rhs, (contract, ((), ())), precision=HIGH)


def apply_rows(data_real, data_imag, both, flipped):
    ahead = (((1,), (0,)))
    return dots(data_real, both, ahead) + dots(data_imag, flipped, ahead)


def ring_place(z, size):
    return jnp.where(z % 2 == 0, z // 2, size - 1 - z // 2)


def ring_owner(place, size):
    return jnp.where(2 * place < size, 2 * place, 2 * (size - 1 - place) + 1)


def ring_neighbours(size):
    z = lax.axis_index("rcv")
    place = ring_place(z, size)
    after = ring_owner((place + 1) % size, size)
    before = ring_owner((place + size - 1) % size, size)
    return z, place, after, before


def greet(freqs, after=None, before=None):
    me = lax.axis_index("freq")
    barrier = pltpu.get_barrier_semaphore()
    waits = freqs - 1
    for k in range(1, freqs):
        pl.semaphore_signal(
            barrier, inc=1, device_id={"freq": (me + k) % freqs}, device_id_type=MESH
        )
    if after is not None:
        for other in (after, before):
            pl.semaphore_signal(barrier, inc=1, device_id={"rcv": other}, device_id_type=MESH)
        waits += 2
    pl.semaphore_wait(barrier, waits)


def start_split(freqs, src, dst, sends, recvs, own):
    me = lax.axis_index("freq")
    rows = dst.shape[2]

    def part(j):
        return src.at[:, 0, pl.ds(pl.multiple_of(j * rows, 8), rows), :]

    copies = []
    for k in range(1, freqs):
        to = (me + k) % freqs
        copies.append(
            pltpu.make_async_remote_copy(
                part(to), dst.at[:, me], sends.at[k], recvs.at[k],
                device_id={"freq": to}, device_id_type=MESH,
            )
        )
    copies.append(pltpu.make_async_copy(part(me), dst.at[:, me], own))
    for copy in copies:
        copy.start()
    return copies


def start_join(freqs, src, dst, sends, recvs, own):
    me = lax.axis_index("freq")
    rows = src.shape[2]
    land = dst.at[:, 0, pl.ds(pl.multiple_of(me * rows, 8), rows), :]
    copies = []
    for k in range(1, freqs):
        to = (me + k) % freqs
        copies.append(
            pltpu.make_async_remote_copy(
                src.at[:, to], land, sends.at[k], recvs.at[k],
                device_id={"freq": to}, device_id_type=MESH,
            )
        )
    copies.append(pltpu.make_async_copy(src.at[:, me], land, own))
    for copy in copies:
        copy.start()
    return copies


def start_rows(freqs, src, dst, sends, recvs, own):
    me = lax.axis_index("freq")
    rows = dst.shape[1]

    def part(j):
        return src.at[pl.ds(pl.multiple_of(j * rows, 8), rows), :]

    copies = []
    for k in range(1, freqs):
        to = (me + k) % freqs
        copies.append(
            pltpu.make_async_remote_copy(
                part(to), dst.at[me], sends.at[k], recvs.at[k],
                device_id={"freq": to}, device_id_type=MESH,
            )
        )
    copies.append(pltpu.make_async_copy(part(me), dst.at[me], own))
    for copy in copies:
        copy.start()
    return copies


def ring_gather(size, place, after, blocks, sends, recvs):
    for step in range(size - 1):
        at = ring_owner((place + size - step) % size, size)
        copy = pltpu.make_async_remote_copy(
            blocks.at[at], blocks.at[at], sends.at[step], recvs.at[step],
            device_id={"rcv": after}, device_id_type=MESH,
        )
        copy.start()
        copy.wait()


def first_body(freqs, size, green, picked, gathered, whole, sends, recvs, own, rsend, rrecv):
    z, place, after, before = ring_neighbours(size)
    whole[z] = picked[...]
    greet(freqs, after, before)
    copies = start_split(freqs, green, gathered, sends, recvs, own)
    ring_gather(size, place, after, whole, rsend, rrecv)
    for copy in copies:
        copy.wait()


def second_body(
    freqs, size, shrunk, adjoint, local, picked, back, dir_all, dir_timed, pick_timed,
    held, total, sends, recvs, own, rsend, rrecv, gsend, grecv, dsend, drecv, down, psend, precv, pown,
):
    me = lax.axis_index("freq")
    z, place, after, before = ring_neighbours(size)
    greet(freqs, after, before)
    copies = start_join(freqs, shrunk, back, sends, recvs, own)
    copies += start_rows(freqs, picked, pick_timed, psend, precv, pown)
    for step in range(size - 1):
        at = ring_owner((place + 2 * size - 1 - step) % size, size)
        if step:
            total[step - 1] = held[step - 1] + adjoint[at]
        copy = pltpu.make_async_remote_copy(
            adjoint.at[at] if step == 0 else total.at[step - 1],
            held.at[step], rsend.at[step], rrecv.at[step],
            device_id={"rcv": after}, device_id_type=MESH,
        )
        copy.start()
        copy.wait()
    dir_all[z] = local[...] - (held[size - 2] + adjoint[z])
    copies += start_rows(freqs, dir_all.at[z], dir_timed, dsend, drecv, down)
    ring_gather(size, place, after, dir_all, gsend, grecv)
    for copy in copies:
        copy.wait()


def third_body(
    freqs, size, level_ref, norms, keep, picks, dirs, out,
    freq_box, rcv_box, cols, fsend, frecv, zsend, zrecv, sends, recvs, own,
):
    me = lax.axis_index("freq")
    z = lax.axis_index("rcv")
    barrier = pltpu.get_barrier_semaphore()
    for k in range(1, freqs):
        pl.semaphore_signal(
            barrier, inc=1, device_id={"freq": (me + k) % freqs}, device_id_type=MESH
        )
    for k in range(1, size):
        pl.semaphore_signal(barrier, inc=1, device_id={"rcv": (z + k) % size}, device_id_type=MESH)
    pl.semaphore_wait(barrier, freqs + size - 2)

    copies = []
    for k in range(1, freqs):
        copies.append(
            pltpu.make_async_remote_copy(
                norms, freq_box.at[k], fsend.at[k], frecv.at[k],
                device_id={"freq": (me + k) % freqs}, device_id_type=MESH,
            )
        )
    for copy in copies:
        copy.start()
    for copy in copies:
        copy.wait()
    parts = norms[...]
    for k in range(1, freqs):
        parts = parts + freq_box[k]
    rcv_box[0] = parts
    copies = []
    for k in range(1, size):
        copies.append(
            pltpu.make_async_remote_copy(
                rcv_box.at[0], rcv_box.at[k], zsend.at[k], zrecv.at[k],
                device_id={"rcv": (z + k) % size}, device_id_type=MESH,
            )
        )
    for copy in copies:
        copy.start()
    for copy in copies:
        copy.wait()
    total = rcv_box[0]
    for k in range(1, size):
        total = total + rcv_box[k]
    step = total[0] / total[1]
    level = level_ref[0]
    count = picks.shape[2] // 2

    def tile(i, carry):
        rows = pl.ds(pl.multiple_of(i * 8, 8), 8)
        for lane in range(0, count, 128):
            re = slice(lane, lane + 128)
            im = slice(count + lane, count + lane + 128)
            points = [
                (
                    picks[f, rows, re] + step * dirs[f, rows, re],
                    picks[f, rows, im] + step * dirs[f, rows, im],
                )
                for f in range(freqs)
            ]
            done = shrink_points(points, keep[:, re], level)
            for f in range(freqs):
                cols[f, rows, re] = done[f][0]
                cols[f, rows, im] = done[f][1]
        return carry

    lax.fori_loop(0, picks.shape[1] // 8, tile, 0)
    rows = cols.shape[1]
    land = out.at[pl.ds(pl.multiple_of(me * rows, 8), rows), :]
    copies = []
    for k in range(1, freqs):
        to = (me + k) % freqs
        copies.append(
            pltpu.make_async_remote_copy(
                cols.at[to], land, sends.at[k], recvs.at[k],
                device_id={"freq": to}, device_id_type=MESH,
            )
        )
    copies.append(pltpu.make_async_copy(cols.at[me], land, own))
    for copy in copies:
        copy.start()
    for copy in copies:
        copy.wait()


ANY = pl.BlockSpec(memory_space=pltpu.HBM)
VMEM = pl.BlockSpec(memory_space=pltpu.VMEM)
DMA = pltpu.SemaphoreType.DMA


def first_call(freqs, size, green, picked):
    two, _, rows, width = green.shape
    return pl.pallas_call(
        functools.partial(first_body, freqs, size),
        out_shape=(
            jax.ShapeDtypeStruct((two, freqs, rows // freqs, width), jnp.float32),
            jax.ShapeDtypeStruct((size,) + picked.shape, jnp.float32),
        ),
        in_specs=[ANY, VMEM],
        out_specs=(ANY, VMEM),
        scratch_shapes=[DMA((freqs,)), DMA((freqs,)), DMA(()), DMA((size,)), DMA((size,))],
        compiler_params=pltpu.CompilerParams(
            collective_id=0, has_side_effects=True, vmem_limit_bytes=40 << 20
        ),
    )(green, picked)


def second_call(freqs, size, shrunk, adjoint, local, picked):
    two, _, part, width = shrunk.shape
    rows, both = local.shape
    pair = [DMA((freqs,)), DMA((freqs,)), DMA(())]
    ring = [DMA((size,)), DMA((size,))]
    return pl.pallas_call(
        functools.partial(second_body, freqs, size),
        out_shape=(
            jax.ShapeDtypeStruct((two, 1, rows, width), jnp.float32),
            jax.ShapeDtypeStruct((size, rows, both), jnp.float32),
            jax.ShapeDtypeStruct((freqs, part, both), jnp.float32),
            jax.ShapeDtypeStruct((freqs, part, both), jnp.float32),
        ),
        in_specs=[ANY, VMEM, VMEM, VMEM],
        out_specs=(ANY, VMEM, VMEM, VMEM),
        scratch_shapes=[
            pltpu.VMEM((size - 1, rows, both), jnp.float32),
            pltpu.VMEM((size - 2, rows, both), jnp.float32),
        ]
        + pair + ring + ring + pair + pair,
        compiler_params=pltpu.CompilerParams(
            collective_id=1, has_side_effects=True, vmem_limit_bytes=48 << 20
        ),
    )(shrunk, adjoint, local, picked)


def third_call(freqs, size, level, norms, keep, picks, dirs):
    _, part, both = picks.shape
    return pl.pallas_call(
        functools.partial(third_body, freqs, size),
        out_shape=jax.ShapeDtypeStruct((part * freqs, both), jnp.float32),
        in_specs=[pl.BlockSpec(memory_space=pltpu.SMEM), VMEM, VMEM, VMEM, VMEM],
        out_specs=VMEM,
        scratch_shapes=[
            pltpu.VMEM((freqs, 2, 8, 128), jnp.float32),
            pltpu.VMEM((size, 2, 8, 128), jnp.float32),
            pltpu.VMEM((freqs, part, both), jnp.float32),
            DMA((freqs,)), DMA((freqs,)), DMA((size,)), DMA((size,)),
            DMA((freqs,)), DMA((freqs,)), DMA(()),
        ],
        compiler_params=pltpu.CompilerParams(
            collective_id=2, has_side_effects=True, vmem_limit_bytes=32 << 20
        ),
    )(level, norms, keep, picks, dirs)


def pick_body(hot_ref, x_ref, o_ref):
    picks = hot_ref.shape[1]
    hot = hot_ref[...]
    for part in range(2):
        x = x_ref[part, 0]
        hi = x.astype(jnp.bfloat16)
        rest = x - hi.astype(jnp.float32)
        mid = rest.astype(jnp.bfloat16)
        low = (rest - mid.astype(jnp.float32)).astype(jnp.bfloat16)
        o_ref[:, part * picks : (part + 1) * picks] = (
            jnp.dot(hi, hot, preferred_element_type=jnp.float32)
            + jnp.dot(mid, hot, preferred_element_type=jnp.float32)
        ) + jnp.dot(low, hot, preferred_element_type=jnp.float32)


def pick_call(hot, green):
    two, one, rows, width = green.shape
    picks = hot.shape[1]
    tile = rows // 4 if rows % 32 == 0 else rows
    return pl.pallas_call(
        pick_body,
        grid=(rows // tile,),
        in_specs=[
            pl.BlockSpec((width, picks), lambda i: (0, 0)),
            pl.BlockSpec((two, one, tile, width), lambda i: (0, 0, i, 0)),
        ],
        out_specs=pl.BlockSpec((tile, 2 * picks), lambda i: (i, 0)),
        out_shape=jax.ShapeDtypeStruct((rows, 2 * picks), jnp.float32),
    )(hot, green)


def on_device(green_freq, data_matrix, shot_panels, wavelet, sources, support, threshold):
    width = green_freq.shape[3]
    rows_here = green_freq.shape[2]
    picks = sources.shape[0]
    keep_all = support.astype(jnp.float32)
    freqs = lax.axis_size("freq")
    size = lax.axis_size("rcv")
    fast = rows_here % (8 * freqs) == 0 and size % 2 == 0 and size > 2
    places = jnp.arange(width, dtype=jnp.int32)
    pickcat = pick_call((places[:, None] == sources[None, :]).astype(jnp.bfloat16), green_freq)
    picked = (pickcat[:, :picks], pickcat[:, picks:])
    if fast:
        gathered, both = first_call(freqs, size, green_freq, pickcat)
        both = both.reshape(size * rows_here, 2 * picks)
    else:
        gathered = lax.all_to_all(green_freq, "freq", split_axis=2, concat_axis=1, tiled=True)
        both = lax.all_gather(pickcat, "rcv", axis=0, tiled=True)
    wr = wavelet[0, 0]
    wi = wavelet[1, 0]
    dr = data_matrix[0, 0]
    di = data_matrix[1, 0]
    flipped = jnp.concatenate([-both[:, picks:], both[:, :picks]], axis=1)
    multiple = apply_rows(dr, di, both, flipped)
    resid_real = shot_panels[0, 0] - (wr * picked[0] - wi * picked[1] - multiple[:, :picks])
    resid_imag = shot_panels[1, 0] - (wr * picked[1] + wi * picked[0] - multiple[:, picks:])
    residual = jnp.stack([resid_real, resid_imag])[:, None]
    down = ((0,), (0,))
    rboth = jnp.concatenate([resid_real, resid_imag], axis=1)
    rflip = jnp.concatenate([resid_imag, -resid_real], axis=1)
    adjoint = dots(dr, rboth, down) + dots(di, rflip, down)
    shrunk = shrink_call(threshold, keep_all, (gathered,))
    local = jnp.concatenate(
        [wr * resid_real + wi * resid_imag, wr * resid_imag - wi * resid_real], axis=1
    )
    if fast:
        back, dir_all, dir_timed, pick_timed = second_call(
            freqs, size, shrunk, adjoint.reshape(size, rows_here, 2 * picks), local, pickcat
        )
        direction = lax.dynamic_index_in_dim(dir_all, lax.axis_index("rcv"), 0, keepdims=False)
        dir_all = dir_all.reshape(size * rows_here, 2 * picks)
    else:
        reduced = lax.psum_scatter(adjoint, "rcv", scatter_dimension=0, tiled=True)
        direction = local - reduced
        dir_all = lax.all_gather(direction, "rcv", axis=0, tiled=True)
        back = lax.all_to_all(shrunk, "freq", split_axis=1, concat_axis=2, tiled=True)
        dir_timed = lax.all_to_all(
            jnp.stack([direction[:, :picks], direction[:, picks:]])[:, None],
            "freq", split_axis=2, concat_axis=1, tiled=True,
        )
    dir_real = direction[:, :picks]
    dir_imag = direction[:, picks:]
    pushed = apply_rows(
        dr, di, dir_all, jnp.concatenate([-dir_all[:, picks:], dir_all[:, :picks]], axis=1)
    )
    image_real = wr * dir_real - wi * dir_imag - pushed[:, :picks]
    image_imag = wr * dir_imag + wi * dir_real - pushed[:, picks:]
    norm_dir = jnp.sum(direction * direction)
    norm_img = jnp.sum(image_real * image_real + image_imag * image_imag)
    keep_cols = jnp.take(keep_all, sources, axis=1)
    norms = jnp.stack([norm_dir, norm_img])
    if fast:
        cols_back = third_call(
            freqs, size, threshold, jnp.broadcast_to(norms[:, None, None], (2, 8, 128)),
            keep_cols, pick_timed, dir_timed,
        )
    else:
        totals = lax.psum(norms, ("freq", "rcv"))
        scalars = jnp.concatenate([threshold, (totals[0] / totals[1])[None]])
        pick_timed = jnp.take(gathered, sources, axis=3)
        cols = shrink_call(scalars, keep_cols, (pick_timed, dir_timed))
        cols_back = lax.all_to_all(cols, "freq", split_axis=1, concat_axis=2, tiled=True)
        cols_back = jnp.concatenate([cols_back[0, 0], cols_back[1, 0]], axis=1)
    hot = sources[:, None] == places[None, :]
    mask = jnp.any(hot, axis=0, keepdims=True).astype(jnp.float32)
    green_next = merge_call(mask, hot.astype(jnp.bfloat16), cols_back, back)
    return (green_next, residual)


def solution(mesh):
    in_specs = (
        P(None, "freq", "rcv", None),
        P(None, "freq", "rcv", None),
        P(None, "freq", "rcv", None),
        P(None, "freq"),
        P(),
        P(),
        P(),
    )
    out_specs = (P(None, "freq", "rcv", None), P(None, "freq", "rcv", None))
    return jax.shard_map(
        on_device, mesh=mesh, in_specs=in_specs, out_specs=out_specs, check_vma=False
    )
```

```python
import functools
import math

import jax
import jax.numpy as jnp
from jax import lax
from jax.experimental import pallas as pl
from jax.experimental.pallas import tpu as pltpu
from jax.sharding import PartitionSpec as P

HIGH = lax.Precision.HIGH
MESH = pl.DeviceIdType.MESH


def transform(points, sign):
    count = len(points)
    if count == 1:
        return points
    if count % 2:
        out = []
        for t in range(count):
            real, imag = points[0]
            for f in range(1, count):
                angle = sign * 2.0 * math.pi * (f * t % count) / count
                c, s = math.cos(angle), math.sin(angle)
                real = real + (c * points[f][0] - s * points[f][1])
                imag = imag + (s * points[f][0] + c * points[f][1])
            out.append((real, imag))
        return out
    even = transform(points[0::2], sign)
    odd = transform(points[1::2], sign)
    low, high = [], []
    for k in range(count // 2):
        er, ei = even[k]
        r, i = odd[k]
        angle = 8 * k / count
        if k == 0:
            tr, ti = r, i
        elif angle == 2:
            tr, ti = (-i, r) if sign > 0 else (i, -r)
        elif angle == 1:
            h = math.sqrt(0.5)
            tr, ti = (h * (r - i), h * (r + i)) if sign > 0 else (h * (r + i), h * (i - r))
        elif angle == 3:
            h = math.sqrt(0.5)
            tr, ti = (-h * (r + i), h * (r - i)) if sign > 0 else (h * (i - r), -h * (r + i))
        else:
            c = math.cos(2 * math.pi * k / count)
            s = sign * math.sin(2 * math.pi * k / count)
            tr, ti = c * r - s * i, s * r + c * i
        low.append((er + tr, ei + ti))
        high.append((er - tr, ei - ti))
    return low + high


def shrink_points(points, keep, level):
    count = len(points)
    timed = transform(points, 1)
    kept = []
    for t, (real, imag) in enumerate(timed):
        size = jnp.sqrt(real * real + imag * imag)
        factor = jnp.maximum(size - level, 0.0) / jnp.maximum(size, level) * keep[t : t + 1]
        factor = factor * (1.0 / count)
        kept.append((factor * real, factor * imag))
    return transform(kept, -1)


def shrink_body(scal_ref, keep_ref, *refs):
    *x_refs, o_ref = refs
    x_ref = x_refs[0]
    count = x_ref.shape[1]
    level = scal_ref[0]

    def lanes(j, carry):
        at = pl.ds(pl.multiple_of(j * 128, 128), 128)
        points = [(x_ref[0, f, :, at], x_ref[1, f, :, at]) for f in range(count)]
        if len(x_refs) == 2:
            d_ref = x_refs[1]
            step = scal_ref[1]
            points = [
                (r + step * d_ref[0, f, :, at], i + step * d_ref[1, f, :, at])
                for f, (r, i) in enumerate(points)
            ]
        out = shrink_points(points, keep_ref[:, at], level)
        for f in range(count):
            o_ref[0, f, :, at] = out[f][0]
            o_ref[1, f, :, at] = out[f][1]
        return carry

    lax.fori_loop(0, x_ref.shape[3] // 128, lanes, 0)


def shrink_call(scalars, keep, arrays):
    two, count, rows, width = arrays[0].shape
    tile = 8 if rows % 8 == 0 else rows
    if rows % 24 == 0 and width <= 512:
        tile = 24
    block = pl.BlockSpec((two, count, tile, width), lambda j: (0, 0, j, 0))
    size = arrays[0].size * 4
    return pl.pallas_call(
        shrink_body,
        grid=(rows // tile,),
        in_specs=[
            pl.BlockSpec(memory_space=pltpu.SMEM),
            pl.BlockSpec((count, width), lambda j: (0, 0)),
        ]
        + [block] * len(arrays),
        out_specs=block,
        out_shape=jax.ShapeDtypeStruct(arrays[0].shape, jnp.float32),
        cost_estimate=pl.CostEstimate(
            flops=40 * arrays[0].size, bytes_accessed=size * (1 + len(arrays)), transcendentals=0
        ),
    )(scalars, keep, *arrays)


def merge_body(mask_ref, hot_ref, cols_ref, back_ref, o_ref):
    hot = hot_ref[...]
    mask = mask_ref[...] > 0.5
    for part in range(2):
        x = cols_ref[:, part * hot.shape[0] : (part + 1) * hot.shape[0]]
        hi = x.astype(jnp.bfloat16)
        rest = x - hi.astype(jnp.float32)
        mid = rest.astype(jnp.bfloat16)
        low = (rest - mid.astype(jnp.float32)).astype(jnp.bfloat16)
        spread = (
            jnp.dot(hi, hot, preferred_element_type=jnp.float32)
            + jnp.dot(mid, hot, preferred_element_type=jnp.float32)
        ) + jnp.dot(low, hot, preferred_element_type=jnp.float32)
        o_ref[part, 0] = jnp.where(mask, spread, back_ref[part, 0])


def merge_call(mask, hot, cols, back):
    two, one, rows, width = back.shape
    picked = hot.shape[0]
    tile = rows // 4 if rows % 32 == 0 else rows
    return pl.pallas_call(
        merge_body,
        grid=(rows // tile,),
        in_specs=[
            pl.BlockSpec((1, width), lambda i: (0, 0)),
            pl.BlockSpec((picked, width), lambda i: (0, 0)),
            pl.BlockSpec((tile, two * picked), lambda i: (i, 0)),
            pl.BlockSpec((two, one, tile, width), lambda i: (0, 0, i, 0)),
        ],
        out_specs=pl.BlockSpec((two, one, tile, width), lambda i: (0, 0, i, 0)),
        out_shape=jax.ShapeDtypeStruct(back.shape, jnp.float32),
    )(mask, hot, cols, back)


def dots(lhs, rhs, contract):
    return lax.dot_general(lhs, rhs, (contract, ((), ())), precision=HIGH)


def apply_rows(data_real, data_imag, both, flipped):
    ahead = (((1,), (0,)))
    return dots(data_real, both, ahead) + dots(data_imag, flipped, ahead)


def ring_place(z, size):
    return jnp.where(z % 2 == 0, z // 2, size - 1 - z // 2)


def ring_owner(place, size):
    return jnp.where(2 * place < size, 2 * place, 2 * (size - 1 - place) + 1)


def ring_neighbours(size):
    z = lax.axis_index("rcv")
    place = ring_place(z, size)
    after = ring_owner((place + 1) % size, size)
    before = ring_owner((place + size - 1) % size, size)
    return z, place, after, before


def greet(freqs, after=None, before=None):
    me = lax.axis_index("freq")
    barrier = pltpu.get_barrier_semaphore()
    waits = freqs - 1
    for k in range(1, freqs):
        pl.semaphore_signal(
            barrier, inc=1, device_id={"freq": (me + k) % freqs}, device_id_type=MESH
        )
    if after is not None:
        for other in (after, before):
            pl.semaphore_signal(barrier, inc=1, device_id={"rcv": other}, device_id_type=MESH)
        waits += 2
    pl.semaphore_wait(barrier, waits)


def start_split(freqs, src, dst, sends, recvs, own):
    me = lax.axis_index("freq")
    rows = dst.shape[2]

    def part(j):
        return src.at[:, 0, pl.ds(pl.multiple_of(j * rows, 8), rows), :]

    copies = []
    for k in range(1, freqs):
        to = (me + k) % freqs
        copies.append(
            pltpu.make_async_remote_copy(
                part(to), dst.at[:, me], sends.at[k], recvs.at[k],
                device_id={"freq": to}, device_id_type=MESH,
            )
        )
    copies.append(pltpu.make_async_copy(part(me), dst.at[:, me], own))
    for copy in copies:
        copy.start()
    return copies


def start_join(freqs, src, dst, sends, recvs, own):
    me = lax.axis_index("freq")
    rows = src.shape[2]
    land = dst.at[:, 0, pl.ds(pl.multiple_of(me * rows, 8), rows), :]
    copies = []
    for k in range(1, freqs):
        to = (me + k) % freqs
        copies.append(
            pltpu.make_async_remote_copy(
                src.at[:, to], land, sends.at[k], recvs.at[k],
                device_id={"freq": to}, device_id_type=MESH,
            )
        )
    copies.append(pltpu.make_async_copy(src.at[:, me], land, own))
    for copy in copies:
        copy.start()
    return copies


def start_rows(freqs, src, dst, sends, recvs, own):
    me = lax.axis_index("freq")
    rows = dst.shape[1]

    def part(j):
        return src.at[pl.ds(pl.multiple_of(j * rows, 8), rows), :]

    copies = []
    for k in range(1, freqs):
        to = (me + k) % freqs
        copies.append(
            pltpu.make_async_remote_copy(
                part(to), dst.at[me], sends.at[k], recvs.at[k],
                device_id={"freq": to}, device_id_type=MESH,
            )
        )
    copies.append(pltpu.make_async_copy(part(me), dst.at[me], own))
    for copy in copies:
        copy.start()
    return copies


def ring_gather(size, place, after, blocks, sends, recvs):
    rows = blocks.shape[0] // size
    for step in range(size - 1):
        at = ring_owner((place + size - step) % size, size)
        part = blocks.at[pl.ds(pl.multiple_of(at * rows, 8), rows), :]
        copy = pltpu.make_async_remote_copy(
            part, part, sends.at[step], recvs.at[step],
            device_id={"rcv": after}, device_id_type=MESH,
        )
        copy.start()
        copy.wait()


def halves(x):
    hi = x.astype(jnp.bfloat16)
    return hi, (x - hi.astype(jnp.float32)).astype(jnp.bfloat16)


def product(lhs, rhs, contract):
    lh, ll = lhs
    rh, rl = rhs

    def dot(x, y):
        return lax.dot_general(x, y, (contract, ((), ())), preferred_element_type=jnp.float32)

    return (dot(lh, rl) + dot(ll, rh)) + dot(lh, rh)


CHUNK = 256


def apply_data(data, x_ref, acc):
    picks = x_ref.shape[1] // 2
    acc[...] = jnp.zeros_like(acc)

    def chunk(i, carry):
        at = pl.ds(pl.multiple_of(i * CHUNK, CHUNK), CHUNK)
        x = x_ref[at, :]
        turned = jnp.concatenate([-x[:, picks:], x[:, :picks]], axis=1)
        acc[...] += product(halves(data[0, :, at]), halves(x), ((1,), (0,)))
        acc[...] += product(halves(data[1, :, at]), halves(turned), ((1,), (0,)))
        return carry

    lax.fori_loop(0, x_ref.shape[0] // CHUNK, chunk, 0)


def apply_adjoint(data, x_ref, out):
    picks = x_ref.shape[1] // 2
    x = x_ref[...]
    straight = halves(x)
    turned = halves(jnp.concatenate([x[:, picks:], -x[:, :picks]], axis=1))

    def chunk(i, carry):
        at = pl.ds(pl.multiple_of(i * CHUNK, CHUNK), CHUNK)
        out[at, :] = product(halves(data[0, :, at]), straight, ((0,), (0,))) + product(
            halves(data[1, :, at]), turned, ((0,), (0,))
        )
        return carry

    lax.fori_loop(0, out.shape[0] // CHUNK, chunk, 0)


def first_body(
    freqs, size, level, wave, green, picked, shots, keep, data_hbm,
    gathered, shrunk, back, residual, norms, dir_timed, pick_timed,
    whole, dir_all, adjoint, local, held, total, data, image,
    fsend, frecv, fown, sends, recvs, own, arsend, arrecv, rsend, rrecv, gsend, grecv,
    dsend, drecv, down, psend, precv, pown, load,
):
    z, place, after, before = ring_neighbours(size)
    rows, both = picked.shape
    picks = both // 2

    def part(at):
        return pl.ds(pl.multiple_of(at * rows, 8), rows)

    fetch = pltpu.make_async_copy(data_hbm.at[:, 0], data, load)
    fetch.start()
    whole[part(z), :] = picked[...]
    greet(freqs, after, before)
    there = start_split(freqs, green, gathered, fsend, frecv, fown)
    ring_gather(size, place, after, whole, arsend, arrecv)
    fetch.wait()
    apply_data(data, whole, residual)
    wr, wi = wave[0], wave[1]
    re, im = slice(0, picks), slice(picks, both)
    rr = shots[:, re] - (wr * picked[:, re] - wi * picked[:, im] - residual[:, re])
    ri = shots[:, im] - (wr * picked[:, im] + wi * picked[:, re] - residual[:, im])
    residual[:, re] = rr
    residual[:, im] = ri
    local[:, re] = wr * rr + wi * ri
    local[:, im] = wr * ri - wi * rr
    apply_adjoint(data, residual, adjoint)
    copies = []
    for step in range(size - 1):
        at = ring_owner((place + 2 * size - 1 - step) % size, size)
        if step:
            total[step - 1] = held[step - 1] + adjoint[part(at), :]
        copy = pltpu.make_async_remote_copy(
            adjoint.at[part(at), :] if step == 0 else total.at[step - 1],
            held.at[step], rsend.at[step], rrecv.at[step],
            device_id={"rcv": after}, device_id_type=MESH,
        )
        copy.start()
        if step == 0:
            for sent in there:
                sent.wait()
            two, count, deep, width = gathered.shape
            block = pl.BlockSpec((two, count, 8, width), lambda j: (0, 0, j, 0))
            pltpu.emit_pipeline(
                lambda x, o: shrink_body(level, keep, x, o),
                grid=(deep // 8,),
                in_specs=[block],
                out_specs=[block],
            )(gathered, shrunk)
            copies += start_join(freqs, shrunk, back, sends, recvs, own)
            copies += start_rows(freqs, picked, pick_timed, psend, precv, pown)
        copy.wait()
    dir_all[part(z), :] = local[...] - (held[size - 2] + adjoint[part(z), :])
    copies += start_rows(freqs, dir_all.at[part(z), :], dir_timed, dsend, drecv, down)
    ring_gather(size, place, after, dir_all, gsend, grecv)
    apply_data(data, dir_all, image)
    mine = dir_all[part(z), :]
    gr = wr * mine[:, re] - wi * mine[:, im] - image[:, re]
    gi = wr * mine[:, im] + wi * mine[:, re] - image[:, im]
    norms[0] = jnp.full((8, 128), jnp.sum(mine * mine))
    norms[1] = jnp.full((8, 128), jnp.sum(gr * gr + gi * gi))
    for copy in copies:
        copy.wait()


def third_body(
    freqs, size, level_ref, norms, keep, picks, dirs, out,
    freq_box, rcv_box, cols, fsend, frecv, zsend, zrecv, sends, recvs, own,
):
    me = lax.axis_index("freq")
    z = lax.axis_index("rcv")
    barrier = pltpu.get_barrier_semaphore()
    for k in range(1, freqs):
        pl.semaphore_signal(
            barrier, inc=1, device_id={"freq": (me + k) % freqs}, device_id_type=MESH
        )
    for k in range(1, size):
        pl.semaphore_signal(barrier, inc=1, device_id={"rcv": (z + k) % size}, device_id_type=MESH)
    pl.semaphore_wait(barrier, freqs + size - 2)

    copies = []
    for k in range(1, freqs):
        copies.append(
            pltpu.make_async_remote_copy(
                norms, freq_box.at[k], fsend.at[k], frecv.at[k],
                device_id={"freq": (me + k) % freqs}, device_id_type=MESH,
            )
        )
    for copy in copies:
        copy.start()
    for copy in copies:
        copy.wait()
    parts = norms[...]
    for k in range(1, freqs):
        parts = parts + freq_box[k]
    rcv_box[0] = parts
    copies = []
    for k in range(1, size):
        copies.append(
            pltpu.make_async_remote_copy(
                rcv_box.at[0], rcv_box.at[k], zsend.at[k], zrecv.at[k],
                device_id={"rcv": (z + k) % size}, device_id_type=MESH,
            )
        )
    for copy in copies:
        copy.start()
    for copy in copies:
        copy.wait()
    total = rcv_box[0]
    for k in range(1, size):
        total = total + rcv_box[k]
    step = total[0] / total[1]
    level = level_ref[0]
    count = picks.shape[2] // 2

    def tile(i, carry):
        rows = pl.ds(pl.multiple_of(i * 8, 8), 8)
        for lane in range(0, count, 128):
            re = slice(lane, lane + 128)
            im = slice(count + lane, count + lane + 128)
            points = [
                (
                    picks[f, rows, re] + step * dirs[f, rows, re],
                    picks[f, rows, im] + step * dirs[f, rows, im],
                )
                for f in range(freqs)
            ]
            done = shrink_points(points, keep[:, re], level)
            for f in range(freqs):
                cols[f, rows, re] = done[f][0]
                cols[f, rows, im] = done[f][1]
        return carry

    lax.fori_loop(0, picks.shape[1] // 8, tile, 0)
    rows = cols.shape[1]
    land = out.at[pl.ds(pl.multiple_of(me * rows, 8), rows), :]
    copies = []
    for k in range(1, freqs):
        to = (me + k) % freqs
        copies.append(
            pltpu.make_async_remote_copy(
                cols.at[to], land, sends.at[k], recvs.at[k],
                device_id={"freq": to}, device_id_type=MESH,
            )
        )
    copies.append(pltpu.make_async_copy(cols.at[me], land, own))
    for copy in copies:
        copy.start()
    for copy in copies:
        copy.wait()


ANY = pl.BlockSpec(memory_space=pltpu.HBM)
VMEM = pl.BlockSpec(memory_space=pltpu.VMEM)
DMA = pltpu.SemaphoreType.DMA


SMEM = pl.BlockSpec(memory_space=pltpu.SMEM)


def first_call(freqs, size, level, wave, green, picked, shots, keep, data):
    two, _, rows, width = green.shape
    both = picked.shape[1]
    deep = rows // freqs
    f32 = jnp.float32
    split = jax.ShapeDtypeStruct((two, freqs, deep, width), f32)
    timed = jax.ShapeDtypeStruct((freqs, deep, both), f32)
    tall = pltpu.VMEM((size * rows, both), f32)
    flat = pltpu.VMEM((rows, both), f32)
    trio = [DMA((freqs,)), DMA((freqs,)), DMA(())]
    ring = [DMA((size,)), DMA((size,))]
    return pl.pallas_call(
        functools.partial(first_body, freqs, size),
        out_shape=(
            split,
            split,
            jax.ShapeDtypeStruct(green.shape, f32),
            jax.ShapeDtypeStruct(picked.shape, f32),
            jax.ShapeDtypeStruct((2, 8, 128), f32),
            timed,
            timed,
        ),
        in_specs=[SMEM, SMEM, ANY, VMEM, VMEM, VMEM, ANY],
        out_specs=(ANY, ANY, ANY, VMEM, VMEM, VMEM, VMEM),
        scratch_shapes=[
            tall, tall, tall, flat,
            pltpu.VMEM((size - 1, rows, both), f32),
            pltpu.VMEM((size - 2, rows, both), f32),
            pltpu.VMEM((two, rows, width), f32),
            flat,
        ]
        + trio + trio + ring + ring + ring + trio + trio + [DMA(())],
        compiler_params=pltpu.CompilerParams(
            collective_id=0, has_side_effects=True, vmem_limit_bytes=60 << 20
        ),
    )(level, wave, green, picked, shots, keep, data)


def third_call(freqs, size, level, norms, keep, picks, dirs):
    _, part, both = picks.shape
    return pl.pallas_call(
        functools.partial(third_body, freqs, size),
        out_shape=jax.ShapeDtypeStruct((part * freqs, both), jnp.float32),
        in_specs=[pl.BlockSpec(memory_space=pltpu.SMEM), VMEM, VMEM, VMEM, VMEM],
        out_specs=VMEM,
        scratch_shapes=[
            pltpu.VMEM((freqs, 2, 8, 128), jnp.float32),
            pltpu.VMEM((size, 2, 8, 128), jnp.float32),
            pltpu.VMEM((freqs, part, both), jnp.float32),
            DMA((freqs,)), DMA((freqs,)), DMA((size,)), DMA((size,)),
            DMA((freqs,)), DMA((freqs,)), DMA(()),
        ],
        compiler_params=pltpu.CompilerParams(
            collective_id=2, has_side_effects=True, vmem_limit_bytes=32 << 20
        ),
    )(level, norms, keep, picks, dirs)


def pick_body(hot_ref, x_ref, o_ref):
    picks = hot_ref.shape[1]
    hot = hot_ref[...]
    for part in range(2):
        x = x_ref[part, 0]
        hi = x.astype(jnp.bfloat16)
        rest = x - hi.astype(jnp.float32)
        mid = rest.astype(jnp.bfloat16)
        low = (rest - mid.astype(jnp.float32)).astype(jnp.bfloat16)
        o_ref[:, part * picks : (part + 1) * picks] = (
            jnp.dot(hi, hot, preferred_element_type=jnp.float32)
            + jnp.dot(mid, hot, preferred_element_type=jnp.float32)
        ) + jnp.dot(low, hot, preferred_element_type=jnp.float32)


def pick_call(hot, green):
    two, one, rows, width = green.shape
    picks = hot.shape[1]
    tile = rows // 4 if rows % 32 == 0 else rows
    return pl.pallas_call(
        pick_body,
        grid=(rows // tile,),
        in_specs=[
            pl.BlockSpec((width, picks), lambda i: (0, 0)),
            pl.BlockSpec((two, one, tile, width), lambda i: (0, 0, i, 0)),
        ],
        out_specs=pl.BlockSpec((tile, 2 * picks), lambda i: (i, 0)),
        out_shape=jax.ShapeDtypeStruct((rows, 2 * picks), jnp.float32),
    )(hot, green)


def on_device(green_freq, data_matrix, shot_panels, wavelet, sources, support, threshold):
    width = green_freq.shape[3]
    rows_here = green_freq.shape[2]
    picks = sources.shape[0]
    keep_all = support.astype(jnp.float32)
    freqs = lax.axis_size("freq")
    size = lax.axis_size("rcv")
    fast = rows_here % (8 * freqs) == 0 and size % 2 == 0 and size > 2
    fast = fast and width % CHUNK == 0 and picks % 128 == 0
    places = jnp.arange(width, dtype=jnp.int32)
    pickcat = pick_call((places[:, None] == sources[None, :]).astype(jnp.bfloat16), green_freq)
    picked = (pickcat[:, :picks], pickcat[:, picks:])
    keep_cols = jnp.take(keep_all, sources, axis=1)
    wr = wavelet[0, 0]
    wi = wavelet[1, 0]
    if fast:
        wave = wavelet[:, 0]
        shots = jnp.concatenate([shot_panels[0, 0], shot_panels[1, 0]], axis=1)
        _, _, back, resid, norms, dir_timed, pick_timed = first_call(
            freqs, size, threshold, wave, green_freq, pickcat, shots, keep_all, data_matrix
        )
        cols_back = third_call(
            freqs, size, threshold, norms, keep_cols, pick_timed, dir_timed
        )
        residual = jnp.stack([resid[:, :picks], resid[:, picks:]])[:, None]
    else:
        gathered = lax.all_to_all(green_freq, "freq", split_axis=2, concat_axis=1, tiled=True)
        both = lax.all_gather(pickcat, "rcv", axis=0, tiled=True)
        dr = data_matrix[0, 0]
        di = data_matrix[1, 0]
        flipped = jnp.concatenate([-both[:, picks:], both[:, :picks]], axis=1)
        multiple = apply_rows(dr, di, both, flipped)
        resid_real = shot_panels[0, 0] - (wr * picked[0] - wi * picked[1] - multiple[:, :picks])
        resid_imag = shot_panels[1, 0] - (wr * picked[1] + wi * picked[0] - multiple[:, picks:])
        residual = jnp.stack([resid_real, resid_imag])[:, None]
        down = ((0,), (0,))
        rboth = jnp.concatenate([resid_real, resid_imag], axis=1)
        rflip = jnp.concatenate([resid_imag, -resid_real], axis=1)
        adjoint = dots(dr, rboth, down) + dots(di, rflip, down)
        local = jnp.concatenate(
            [wr * resid_real + wi * resid_imag, wr * resid_imag - wi * resid_real], axis=1
        )
        direction = local - lax.psum_scatter(adjoint, "rcv", scatter_dimension=0, tiled=True)
        dir_all = lax.all_gather(direction, "rcv", axis=0, tiled=True)
        shrunk = shrink_call(threshold, keep_all, (gathered,))
        back = lax.all_to_all(shrunk, "freq", split_axis=1, concat_axis=2, tiled=True)
        dir_real = direction[:, :picks]
        dir_imag = direction[:, picks:]
        dir_timed = lax.all_to_all(
            jnp.stack([dir_real, dir_imag])[:, None],
            "freq", split_axis=2, concat_axis=1, tiled=True,
        )
        pushed = apply_rows(
            dr, di, dir_all, jnp.concatenate([-dir_all[:, picks:], dir_all[:, :picks]], axis=1)
        )
        image_real = wr * dir_real - wi * dir_imag - pushed[:, :picks]
        image_imag = wr * dir_imag + wi * dir_real - pushed[:, picks:]
        norm_dir = jnp.sum(direction * direction)
        norm_img = jnp.sum(image_real * image_real + image_imag * image_imag)
        totals = lax.psum(jnp.stack([norm_dir, norm_img]), ("freq", "rcv"))
        scalars = jnp.concatenate([threshold, (totals[0] / totals[1])[None]])
        pick_timed = jnp.take(gathered, sources, axis=3)
        cols = shrink_call(scalars, keep_cols, (pick_timed, dir_timed))
        cols_back = lax.all_to_all(cols, "freq", split_axis=1, concat_axis=2, tiled=True)
        cols_back = jnp.concatenate([cols_back[0, 0], cols_back[1, 0]], axis=1)
    hot = sources[:, None] == places[None, :]
    mask = jnp.any(hot, axis=0, keepdims=True).astype(jnp.float32)
    green_next = merge_call(mask, hot.astype(jnp.bfloat16), cols_back, back)
    return (green_next, residual)


def solution(mesh):
    in_specs = (
        P(None, "freq", "rcv", None),
        P(None, "freq", "rcv", None),
        P(None, "freq", "rcv", None),
        P(None, "freq"),
        P(),
        P(),
        P(),
    )
    out_specs = (P(None, "freq", "rcv", None), P(None, "freq", "rcv", None))
    return jax.shard_map(
        on_device, mesh=mesh, in_specs=in_specs, out_specs=out_specs, check_vma=False
    )
```
